32 devices in a mesh: clip: 2 (over x), trow: 8 (over z, y), tcol: 2 (over core).
Axes of the slice: x: 2, y: 2, z: 4, core: 2. Of those that a mesh axis runs over, the one named last changes fastest.
Arguments:
- field: bfloat16 [8, 2048, 8192], P(None, ('clip', 'trow'), 'tcol'), parts along dimension 1, may hold values from -6 to 6
- pointwise: bfloat16 [2, 8, 8], replicated, may hold values from -2 to 2
- mixing: bfloat16 [2, 2, 8, 8, 4608], replicated, may hold values from -2 to 2
- project: bfloat16 [8], replicated, may hold values from -2 to 2
Outputs:
- image: bfloat16 [2048, 8192], P(('clip', 'trow'), 'tcol'), parts along dimension 0
The draws below stay inside these ranges and needn't reach their ends.
There are 2 independent parts, one for each index of `clip`. The reference program is written for one: setup_inputs(seed, part) draws one part's arguments, and reference() takes and returns one part's arrays. A program takes and returns all parts, laid end to end along the dimension named above; an argument that names none is the same for every part. Nothing has to cross between parts.
All inputs are finite; a program needn't handle non-finite values.
Results may differ from the reference program's by a relative error of at most 0.0084.
Values sent between devices are 32-bit elements; how exact they have to be, the bound alone decides.
A program may use at most 128 MiB of HBM per device.

```python
import math
import jax
import jax.numpy as jnp
from jax import lax

C = 8
NY = 8192
KY = 48
LAYERS = 2
ROW_DEV = 128
MODES2 = 4608
NX = 1024
N_TROW = 8


def block_scale(key, shape, cuts, smallest, high):
    gain = 1.0
    for dim, shards_of in cuts:
        steps = jax.random.uniform(jax.random.fold_in(jax.random.fold_in(key, 6), dim), (shards_of,), jnp.float32, smallest / len(cuts), high / len(cuts))
        gain = gain * jnp.repeat(jnp.exp(steps), shape[dim] // shards_of).reshape((-1,) + (1,) * (len(shape) - 1 - dim))
    return gain


def bell_draw(key, shape, deviation, limit, shards=(), held_as=jnp.bfloat16):
    values = deviation * jax.random.normal(key, shape, jnp.float32)
    if shards:
        values = values * block_scale(key, shape, shards, -0.22, 0.18)
    return jnp.clip(values, -limit, limit).astype(held_as)


def setup_inputs(seed: int = 0, part: int = 0) -> dict:
    keys = jax.random.split(jax.random.key(seed), 5)
    part_splits = jax.random.split(jax.random.fold_in(keys[4], part), 5)
    return {
        "field": bell_draw(part_splits[0], (C, NX, NY), 1.0, 6.0, ((1, 8), (2, 2))),
        "pointwise": bell_draw(keys[1], (LAYERS, C, C), C ** -0.5, 2.0),
        "mixing": bell_draw(keys[2], (LAYERS, 2, C, C, MODES2), C ** -0.5, 2.0),
        "project": bell_draw(keys[3], (C,), C ** -0.5, 2.0),
    }


def column_table(start, count, total, modes):
    columns = start + jnp.arange(count, dtype=jnp.int32)
    freqs = jnp.arange(modes, dtype=jnp.int32)
    phase = columns[:, None] * freqs[None, :] % total
    angle = phase.astype(jnp.float32) * (2.0 * math.pi / total)
    return jnp.concatenate([jnp.cos(angle), -jnp.sin(angle)], axis=1).astype(jnp.bfloat16)

def row_tables(start, count, total, modes):
    rows_here = start + jnp.arange(count, dtype=jnp.int32)
    freqs = jnp.arange(2 * modes, dtype=jnp.int32)
    freqs = jnp.where(freqs < modes, freqs, freqs + (total - 2 * modes)).astype(jnp.int32)
    phase = freqs[:, None] * rows_here[None, :] % total
    angle = phase.astype(jnp.float32) * (2.0 * math.pi / total)
    return (jnp.cos(angle), jnp.sin(angle))

def forward_spectrum(values, row_start, total_rows, col_start, total_cols, modes):
    channels, rows_here, cols_here = values.shape
    table = column_table(col_start, cols_here, total_cols, modes)
    partial_value = jnp.dot(values.reshape(channels * rows_here, cols_here), table, preferred_element_type=jnp.float32)
    partial_value = partial_value.reshape(channels, rows_here, 2 * modes).transpose(1, 0, 2).reshape(rows_here, channels * 2 * modes)
    cosine, sine = row_tables(row_start, rows_here, total_rows, modes)
    stacked = jnp.dot(jnp.concatenate([cosine, sine], axis=0), partial_value, precision=lax.Precision.HIGHEST, preferred_element_type=jnp.float32)
    stacked = stacked.reshape(2, 2 * modes, channels, 2, modes)
    real_part = stacked[0, :, :, 0] + stacked[1, :, :, 1]
    imag_part = stacked[0, :, :, 1] - stacked[1, :, :, 0]
    spectrum = jnp.stack([real_part, imag_part]).transpose(0, 2, 1, 3).reshape(2, channels, 2 * modes * modes)
    return spectrum * (1.0 / math.sqrt(total_rows * total_cols))

def mix_modes(spectrum, weights_in):
    weights = weights_in.astype(jnp.float32)
    real_part = lax.optimization_barrier(jnp.sum(weights[0] * spectrum[0][None], axis=1)) - lax.optimization_barrier(jnp.sum(weights[1] * spectrum[1][None], axis=1))
    imag_part = lax.optimization_barrier(jnp.sum(weights[0] * spectrum[1][None], axis=1)) + lax.optimization_barrier(jnp.sum(weights[1] * spectrum[0][None], axis=1))
    return jnp.stack([real_part, imag_part])

def inverse_field(mixed, row_start, rows_here, total_rows, col_start, cols_here, total_cols, modes):
    channels = mixed.shape[1]
    arranged = mixed.reshape(2, channels, 2 * modes, modes).transpose(2, 0, 1, 3).reshape(2 * modes, 2 * channels * modes)
    cosine, sine = row_tables(row_start, rows_here, total_rows, modes)
    table = jnp.concatenate([cosine.T, sine.T], axis=0)
    stacked = jnp.dot(table, arranged, precision=lax.Precision.HIGHEST, preferred_element_type=jnp.float32)
    stacked = stacked.reshape(2, rows_here, 2, channels, modes)
    real_part = stacked[0, :, 0] - stacked[1, :, 1]
    imag_part = stacked[1, :, 0] + stacked[0, :, 1]
    hidden = jnp.stack([real_part, imag_part], axis=2).transpose(1, 0, 2, 3).reshape(channels * rows_here, 2 * modes).astype(jnp.bfloat16)
    col_tab = column_table(col_start, cols_here, total_cols, modes)
    values = jnp.dot(hidden, col_tab.T, preferred_element_type=jnp.float32) * (1.0 / modes)
    return values.reshape(channels, rows_here, cols_here)

def layer_update(values, weights, mixed, row_start, total_rows, col_start, total_cols, modes):
    channels, rows_here, cols_here = values.shape
    spectral = inverse_field(mixed, row_start, rows_here, total_rows, col_start, cols_here, total_cols, modes)
    local = jnp.dot(weights, values.reshape(channels, rows_here * cols_here), preferred_element_type=jnp.float32)
    return jnp.tanh(local.reshape(channels, rows_here, cols_here) + spectral)

def reference(field, pointwise, mixing, project):
    total_rows = ROW_DEV * N_TROW
    current = field
    result = None
    for layer in range(LAYERS):

        def add_block(carry, index):
            start = (index * ROW_DEV).astype(jnp.int32)
            piece = lax.dynamic_slice_in_dim(current, start, ROW_DEV, 1)
            return (carry + forward_spectrum(piece, start, total_rows, 0, NY, KY), None)
        empty = jnp.zeros((2, C, MODES2), jnp.float32)
        spectrum, ignored = lax.scan(add_block, empty, jnp.arange(N_TROW, dtype=jnp.int32))
        mixed = mix_modes(spectrum, mixing[layer])
        last = layer + 1 == LAYERS

        def one_block(index):
            start = (index * ROW_DEV).astype(jnp.int32)
            piece = lax.dynamic_slice_in_dim(current, start, ROW_DEV, 1)
            updated = layer_update(piece, pointwise[layer], mixed, start, total_rows, 0, NY, KY)
            if last:
                return lax.optimization_barrier(jnp.sum(project.astype(jnp.float32)[:, None, None] * updated, axis=0)).astype(jnp.bfloat16)
            return updated.astype(jnp.bfloat16)
        pieces = lax.map(one_block, jnp.arange(N_TROW, dtype=jnp.int32))
        if last:
            result = pieces.reshape(total_rows, NY)
        else:
            current = pieces.transpose(1, 0, 2, 3).reshape(C, total_rows, NY)
    return result
```

```python
import functools
import math

import jax
import jax.numpy as jnp
import numpy as np
from jax import lax
from jax.experimental import pallas as pl
from jax.experimental.pallas import tpu as pltpu
from jax.sharding import PartitionSpec as P

KY = 48
LAYERS = 2
LANES = 128
HALVES = 2
QUAD = 4
TRIO = 3
XB = 32
MESH = pl.DeviceIdType.MESH
VMEM_BYTES = 62 * 1024 * 1024
BF16, F32 = jnp.bfloat16, jnp.float32
NT = (((1,), (1,)), ((), ()))


def column_constant(total, cores):
    columns = np.arange(total, dtype=np.int64)
    phase = np.arange(KY, dtype=np.int64)[:, None] * columns[None, :] % total
    angle = (phase.astype(np.float32) * np.float32(2.0 * math.pi / total)).astype(np.float64)
    table = np.concatenate([np.cos(angle), -np.sin(angle)], axis=0).astype(np.float32)
    return table.reshape(2 * KY, cores, total // cores).transpose(1, 0, 2).astype(jnp.bfloat16)


def row_constants(total, rows, groups, owners, per, sub):
    index = np.arange(owners)[:, None] * per + np.arange(sub)[None, :]
    valid = (np.arange(sub)[None, :] < per).repeat(owners, 0).reshape(-1)
    index = index.reshape(-1)
    freqs = np.where(index < KY, index, index - 2 * KY)
    keep = valid.astype(np.float64)

    def both(places):
        angle = 2.0 * math.pi * ((freqs[None, :] * places[:, None]) % total) / total
        return np.cos(angle) * keep, np.sin(angle) * keep

    fine = np.stack(both(np.arange(rows, dtype=np.int64))).astype(np.float32)
    coarse = np.stack(both(np.arange(groups, dtype=np.int64) * rows), axis=1)
    coarse = np.pad(coarse, ((0, 0), (0, 6), (0, 0))).astype(np.float32)
    return fine, coarse


def split(value):
    high = value.astype(BF16)
    return high, (value - high.astype(F32)).astype(BF16)


def turned(value):
    lane = lax.broadcasted_iota(jnp.int32, value.shape, 1)
    up = pltpu.roll(value, LANES - KY, 1)
    down = pltpu.roll(value, KY, 1)
    return jnp.where(lane < KY, up, jnp.where(lane < 2 * KY, -down, 0.0))


def pack(parts):
    lane = lax.broadcasted_iota(jnp.int32, parts[0].shape, 1)
    return [
        jnp.where(lane < 2 * KY, parts[j], pltpu.roll(parts[TRIO], 2 * KY - 32 * j, 1)) for j in range(TRIO)
    ]


def unpack(rows):
    lane = lax.broadcasted_iota(jnp.int32, rows[0].shape, 1)
    fourth = jnp.where(
        lane < 32,
        pltpu.roll(rows[0], 32, 1),
        jnp.where(lane < 64, pltpu.roll(rows[1], 64, 1), pltpu.roll(rows[2], 96, 1)),
    )
    return [jnp.where(lane < 2 * KY, r, 0.0) for r in [*rows, fourth]]


def two_transforms(table, first, second):
    value = jnp.concatenate([first, second], axis=1)
    other = jnp.concatenate([turned(first), turned(second)], axis=1)
    high, low = split(jnp.concatenate([value, other], axis=0))
    both = jnp.dot(table, jnp.concatenate([high, low, high], axis=0), preferred_element_type=F32)
    return both[:, :LANES], both[:, LANES:]


def tile_of(cols):
    for size in (2048, 1024, 512, 256, 128):
        if cols % size == 0:
            return size
    return cols


def kernel(
    plan,
    field_hbm, point_hbm, mixing_hbm, project_hbm, et_hbm, fine_hbm, coarse_hbm,
    image_hbm,
    value, local, et, fine, coarse, point, project, raw, same, cross, kron, ahead, back, acc, hidden, total_image, image,
    packed, partner, mine, arrived, spread,
    field_sem, load_sem, pair_send, pair_recv, sum_send, sum_recv, mix_send, mix_recv, relay_send, relay_recv,
):
    groups, cores, owners, first_owner, per, sub, window, scale = plan
    channels, rows, cols = value.shape
    half_channels = channels // HALVES
    tile = tile_of(cols)
    local_tile = min(tile, 512)
    clip = lax.axis_index("clip")
    row = lax.axis_index("trow")
    core = lax.axis_index("tcol")
    other = 1 - core
    near = jnp.clip(row - first_owner, 0, owners - 1)
    is_owner = jnp.logical_and(row >= first_owner, row < first_owner + owners)
    block = core * owners + near
    start_mode = block * (per * KY)
    offset = lax.rem(start_mode, LANES)
    window_start = pl.multiple_of(start_mode - offset, LANES)

    loads = [
        pltpu.make_async_copy(fine_hbm, fine, load_sem.at[0]),
        pltpu.make_async_copy(coarse_hbm.at[row], coarse, load_sem.at[1]),
        pltpu.make_async_copy(et_hbm.at[core], et.at[pl.ds(0, 2 * KY)], load_sem.at[2]),
        pltpu.make_async_copy(point_hbm, point, load_sem.at[3]),
        pltpu.make_async_copy(project_hbm, project, load_sem.at[4]),
        pltpu.make_async_copy(mixing_hbm.at[:, :, :, :, pl.ds(window_start, window)], raw, load_sem.at[5]),
    ]
    for copy in loads[:3]:
        copy.start()

    def field_copy(c):
        return pltpu.make_async_copy(field_hbm.at[c], value.at[c], field_sem.at[c])

    for c in range(channels):
        field_copy(c).start()
    for copy in loads[3:]:
        copy.start()

    arrived[...] = jnp.zeros_like(arrived)
    spread[...] = jnp.zeros_like(spread)
    et[2 * KY :, :] = jnp.zeros((LANES - 2 * KY, cols), BF16)

    barrier = pltpu.get_barrier_semaphore()
    pl.semaphore_signal(barrier, inc=1, device_id=(clip, row, other), device_id_type=MESH)
    for j in range(1, groups):
        peer = lax.rem(row + j, groups)
        pl.semaphore_signal(barrier, inc=1, device_id=(clip, peer, core), device_id_type=MESH)

    def used(ref):
        return ref.at[:, pl.ds(0, per), :]

    loads[0].wait()
    loads[1].wait()
    cc, cs = coarse[0:1, :], coarse[1:2, :]
    cosine = cc * fine[0] - cs * fine[1]
    sine = cs * fine[0] + cc * fine[1]
    high, low = split(jnp.concatenate([cosine, -sine], axis=1))
    back[...] = jnp.concatenate([high, high, low], axis=1)
    high, low = split(jnp.concatenate([cosine.T, sine.T], axis=1) * scale)
    ahead[...] = jnp.concatenate([high, high, low], axis=1)
    loads[2].wait()

    def columns_of(c):
        acc[c] = lax.dot_general(value[c], et[...], NT, preferred_element_type=F32)

    def pair_copy(layer, half):
        return pltpu.make_async_remote_copy(
            src_ref=packed.at[layer, half, other],
            dst_ref=partner.at[layer, half],
            send_sem=pair_send.at[layer, half],
            recv_sem=pair_recv.at[layer, half],
            device_id=(clip, row, other),
            device_id_type=MESH,
        )

    def transform_rows(layer, half):
        parts = []
        for p in range(0, half_channels, 2):
            c = half * half_channels + p
            parts.extend(two_transforms(ahead[...], acc[c], acc[c + 1]))
        for j, rows_j in enumerate(pack(parts)):
            packed[layer, half, :, :, j] = rows_j.reshape(cores, owners, sub, LANES)
        pair_copy(layer, half).start()

    def sum_target(j):
        return lax.rem(near + owners // 2 + j, owners)

    def sum_copy(layer, half, j):
        q = sum_target(j)
        slot = lax.rem(row - (first_owner + q) + groups, groups) - 1
        slot = jnp.maximum(slot, 0)
        return pltpu.make_async_remote_copy(
            src_ref=used(mine.at[layer, half, q]),
            dst_ref=used(arrived.at[layer, half, slot]),
            send_sem=sum_send.at[layer, half, j],
            recv_sem=sum_recv.at[layer, half, slot],
            device_id=(clip, first_owner + q, core),
            device_id_type=MESH,
        )

    def scatter_sums(layer, half):
        pair_copy(layer, half).wait_recv()
        mine[layer, half] = packed[layer, half, core] + partner[layer, half]
        for j in range(owners):
            @pl.when(first_owner + sum_target(j) != row)
            def _():
                sum_copy(layer, half, j).start()

    def spread_copy(layer, half, j):
        return pltpu.make_async_remote_copy(
            src_ref=used(spread.at[layer, half, core, near]),
            dst_ref=used(spread.at[layer, half, core, near]),
            send_sem=mix_send.at[layer, half, j - 1],
            recv_sem=mix_recv.at[layer, half, near],
            device_id=(clip, lax.rem(row + j, groups), core),
            device_id_type=MESH,
        )

    def relay_copy(layer, half, q):
        return pltpu.make_async_remote_copy(
            src_ref=used(spread.at[layer, half, core, q]),
            dst_ref=used(spread.at[layer, half, core, q]),
            send_sem=relay_send.at[layer, half, q],
            recv_sem=relay_recv.at[layer, half, q],
            device_id=(clip, row, other),
            device_id_type=MESH,
        )

    def block_arrival(layer, half, q):
        return pltpu.make_async_remote_copy(
            src_ref=used(spread.at[layer, half, core, q]),
            dst_ref=used(spread.at[layer, half, core, q]),
            send_sem=mix_send.at[layer, half, 0],
            recv_sem=mix_recv.at[layer, half, q],
            device_id=(clip, row, other),
            device_id_type=MESH,
        )

    def partner_arrival(layer, half, q):
        return pltpu.make_async_remote_copy(
            src_ref=used(spread.at[layer, half, other, q]),
            dst_ref=used(spread.at[layer, half, other, q]),
            send_sem=relay_send.at[layer, half, q],
            recv_sem=relay_recv.at[layer, half, q],
            device_id=(clip, row, other),
            device_id_type=MESH,
        )

    def sum_arrival(layer, half, slot):
        return pltpu.make_async_remote_copy(
            src_ref=used(arrived.at[layer, half, slot]),
            dst_ref=used(arrived.at[layer, half, slot]),
            send_sem=sum_send.at[layer, half, 0],
            recv_sem=sum_recv.at[layer, half, slot],
            device_id=(clip, row, other),
            device_id_type=MESH,
        )

    order = sorted(range(1, groups), key=lambda j: abs(2 * j - groups))

    def mix(layer):
        @pl.when(is_owner)
        def _():
            plain = []
            for half in range(HALVES):
                sums = mine[layer, half, near]
                for slot in range(groups - 1):
                    sum_arrival(layer, half, slot).wait_recv()
                    sums = sums + arrived[layer, half, slot]
                plain.extend(unpack([sums[j] for j in range(TRIO)]))
            lane = lax.broadcasted_iota(jnp.int32, plain[0].shape, 1)
            swapped = [
                jnp.where(lane < KY, pltpu.roll(s, LANES - KY, 1), pltpu.roll(s, KY, 1)) for s in plain
            ]
            for half in range(HALVES):
                mixed = []
                for o in range(half * half_channels, (half + 1) * half_channels):
                    at = (layer * channels + o) * channels
                    result = same[at] * plain[0] + cross[at] * swapped[0]
                    for c in range(1, channels):
                        result = result + (same[at + c] * plain[c] + cross[at + c] * swapped[c])
                    mixed.append(result)
                for j, rows_j in enumerate(pack(mixed)):
                    spread[layer, half, core, near, j, 0:per, :] = rows_j[:per]
                for j in order:
                    spread_copy(layer, half, j).start()
                relay_copy(layer, half, near).start()

    def relay(layer, half):
        for q in range(owners):
            @pl.when(first_owner + q != row)
            def _():
                block_arrival(layer, half, q).wait_recv()
                relay_copy(layer, half, q).start()

    def prepare_hidden(layer, half):
        for q in range(owners):
            partner_arrival(layer, half, q).wait_recv()
        parts = unpack([spread[layer, half, :, :, j].reshape(cores * owners * sub, LANES) for j in range(TRIO)])
        for p in range(0, half_channels, 2):
            for k, part in enumerate(two_transforms(back[...], parts[p], parts[p + 1])):
                hidden[half * half_channels + p + k] = part.astype(BF16)

    def kron_matrix(layer):
        size = channels * XB
        spot = lax.broadcasted_iota(jnp.int32, (size, channels), 0) // XB
        pick = (spot == lax.broadcasted_iota(jnp.int32, (size, channels), 1)).astype(F32).astype(BF16)
        wide = jnp.dot(pick, point[layer], preferred_element_type=F32).astype(BF16)
        full = lax.dot_general(wide, pick, NT, preferred_element_type=F32)
        at = lax.rem(lax.broadcasted_iota(jnp.int32, (size, size), 0), XB)
        to = lax.rem(lax.broadcasted_iota(jnp.int32, (size, size), 1), XB)
        kron[layer] = jnp.where(at == to, full, 0.0).astype(BF16)

    def mix_channels(layer):
        def step(i, carry):
            at = pl.multiple_of(i * local_tile, local_tile)
            for b in range(rows // XB):
                piece = value[:, b * XB : (b + 1) * XB, pl.ds(at, local_tile)].reshape(channels * XB, local_tile)
                result = jnp.dot(kron[layer], piece, preferred_element_type=F32)
                local[:, b * XB : (b + 1) * XB, pl.ds(at, local_tile)] = result.reshape(channels, XB, local_tile)
            return carry
        lax.fori_loop(0, cols // local_tile, step, 0)

    def updated(half, at):
        mine_here = slice(half * half_channels, (half + 1) * half_channels)
        lhs = hidden[mine_here].reshape(half_channels * rows, LANES)
        spectral = jnp.dot(lhs, et[:, pl.ds(at, tile)], preferred_element_type=F32)
        spectral = spectral.reshape(half_channels, rows, tile)
        return jnp.tanh(local[mine_here, :, pl.ds(at, tile)] + spectral * (1.0 / KY))

    def update(half):
        def step(i, carry):
            at = pl.multiple_of(i * tile, tile)
            value[half * half_channels : (half + 1) * half_channels, :, pl.ds(at, tile)] = updated(half, at).astype(BF16)
            return carry
        lax.fori_loop(0, cols // tile, step, 0)

    def project_half(half):
        gains = project[...].astype(F32)

        def step(i, carry):
            at = pl.multiple_of(i * tile, tile)
            result = updated(half, at)
            total = None if half == 0 else total_image[:, pl.ds(at, tile)]
            for k in range(half_channels):
                c = half * half_channels + k
                term = gains[0:1, c : c + 1] * result[k]
                total = term if total is None else total + term
            if half + 1 < HALVES:
                total_image[:, pl.ds(at, tile)] = total
            else:
                image[:, pl.ds(at, tile)] = total.astype(BF16)
            return carry
        lax.fori_loop(0, cols // tile, step, 0)

    def prepare_weights():
        loads[5].wait()
        count = LAYERS * 2 * channels
        flat = raw[...].astype(F32).reshape(count * channels, window).astype(BF16)
        mode = lax.broadcasted_iota(jnp.int32, (window, 2 * LANES), 0) - offset
        lane = lax.broadcasted_iota(jnp.int32, (window, 2 * LANES), 1)
        which = lane // LANES
        spot = lane - which * LANES
        wanted = which * KY + jnp.where(spot < KY, spot, spot - KY)
        wanted = jnp.where(spot < 2 * KY, wanted, -window * LANES)
        side = lax.broadcasted_iota(jnp.int32, (LAYERS * channels * channels, LANES), 1)
        for k in range(0, per, 2):
            choose = (mode - k * KY == wanted).astype(F32).astype(BF16)
            picked = jnp.dot(flat, choose, preferred_element_type=F32)
            picked = picked.reshape(LAYERS, 2, channels * channels, 2 * LANES)
            for n in range(2):
                lanes = slice(n * LANES, (n + 1) * LANES)
                real = picked[:, 0, :, lanes].reshape(LAYERS * channels * channels, LANES)
                imag = picked[:, 1, :, lanes].reshape(LAYERS * channels * channels, LANES)
                same[:, k + n, :] = real
                cross[:, k + n, :] = jnp.where(side < KY, -imag, imag)

    def load_and_transform(c, carry):
        field_copy(c).wait()
        columns_of(c)
        return carry

    def transform_only(c, carry):
        columns_of(c)
        return carry

    lax.fori_loop(0, half_channels, load_and_transform, 0)
    pl.semaphore_wait(barrier, groups)
    transform_rows(0, 0)
    lax.fori_loop(half_channels, channels, load_and_transform, 0)
    scatter_sums(0, 0)
    transform_rows(0, 1)
    loads[3].wait()
    loads[4].wait()
    for layer in range(LAYERS):
        kron_matrix(layer)
    scatter_sums(0, 1)
    prepare_weights()

    for layer in range(LAYERS):
        last = layer + 1 == LAYERS
        if last:
            mix_channels(layer)
        mix(layer)
        if not last:
            mix_channels(layer)
        relay(layer, 0)
        prepare_hidden(layer, 0)
        if last:
            project_half(0)
            relay(layer, 1)
            prepare_hidden(layer, 1)
            project_half(1)
        else:
            update(0)
            relay(layer, 1)
            lax.fori_loop(0, half_channels, transform_only, 0)
            transform_rows(layer + 1, 0)
            prepare_hidden(layer, 1)
            update(1)
            scatter_sums(layer + 1, 0)
            lax.fori_loop(half_channels, channels, transform_only, 0)
            transform_rows(layer + 1, 1)
            scatter_sums(layer + 1, 1)

    out = pltpu.make_async_copy(image, image_hbm, load_sem.at[6])
    out.start()
    for layer in range(LAYERS):
        for half in range(HALVES):
            pair_copy(layer, half).wait_send()
            for j in range(owners):
                @pl.when(first_owner + sum_target(j) != row)
                def _():
                    sum_copy(layer, half, j).wait_send()
            for q in range(owners):
                relay_copy(layer, half, q).wait_send()

            @pl.when(is_owner)
            def _():
                for j in order:
                    spread_copy(layer, half, j).wait_send()
    out.wait()


def body(groups, cores, field, pointwise, mixing, project):
    channels, rows, cols = field.shape
    owners = min(4, groups)
    first_owner = (groups - owners) // 2
    per = 2 * KY // (owners * cores)
    sub = -(-per // 8) * 8
    total_rows, total_cols = rows * groups, cols * cores
    scale = 1.0 / math.sqrt(total_rows * total_cols)
    modes = per * KY
    window = max(-(-(b * modes % LANES + modes) // LANES) * LANES for b in range(owners * cores))
    plan = (groups, cores, owners, first_owner, per, sub, window, scale)
    et = jnp.asarray(column_constant(total_cols, cores))
    fine, coarse = row_constants(total_rows, rows, groups, owners * cores, per, sub)
    fine, coarse = jnp.asarray(fine), jnp.asarray(coarse)

    hbm = pl.BlockSpec(memory_space=pl.ANY)
    dma = pltpu.SemaphoreType.DMA
    links = max(groups - 1, 1)
    chunk = (TRIO, sub, LANES)
    pairs = LAYERS * channels * channels
    return pl.pallas_call(
        functools.partial(kernel, plan),
        out_shape=jax.ShapeDtypeStruct((rows, cols), BF16),
        in_specs=[hbm] * 7,
        out_specs=hbm,
        scratch_shapes=[
            pltpu.VMEM((channels, rows, cols), BF16),
            pltpu.VMEM((channels, rows, cols), F32),
            pltpu.VMEM((LANES, cols), BF16),
            pltpu.VMEM(fine.shape, F32),
            pltpu.VMEM(coarse.shape[1:], F32),
            pltpu.VMEM(pointwise.shape, BF16),
            pltpu.VMEM((1, channels), BF16),
            pltpu.VMEM(mixing.shape[:-1] + (window,), BF16),
            pltpu.VMEM((pairs, sub, LANES), F32),
            pltpu.VMEM((pairs, sub, LANES), F32),
            pltpu.VMEM((LAYERS, channels * XB, channels * XB), BF16),
            pltpu.VMEM((cores * owners * sub, 6 * rows), BF16),
            pltpu.VMEM((rows, 6 * cores * owners * sub), BF16),
            pltpu.VMEM((channels, rows, LANES), F32),
            pltpu.VMEM((channels, rows, LANES), BF16),
            pltpu.VMEM((rows, cols), F32),
            pltpu.VMEM((rows, cols), BF16),
            pltpu.VMEM((LAYERS, HALVES, cores, owners) + chunk, F32),
            pltpu.VMEM((LAYERS, HALVES, owners) + chunk, F32),
            pltpu.VMEM((LAYERS, HALVES, owners) + chunk, F32),
            pltpu.VMEM((LAYERS, HALVES, links) + chunk, F32),
            pltpu.VMEM((LAYERS, HALVES, cores, owners) + chunk, F32),
            dma((channels,)), dma((7,)),
            dma((LAYERS, HALVES)), dma((LAYERS, HALVES)),
            dma((LAYERS, HALVES, owners)), dma((LAYERS, HALVES, links)),
            dma((LAYERS, HALVES, links)), dma((LAYERS, HALVES, owners)),
            dma((LAYERS, HALVES, owners)), dma((LAYERS, HALVES, owners)),
        ],
        compiler_params=pltpu.CompilerParams(
            collective_id=0, has_side_effects=True, vmem_limit_bytes=VMEM_BYTES
        ),
        name="operator",
    )(field, pointwise, mixing, project.reshape(1, channels), et, fine, coarse)


def solution(mesh):
    groups, cores = mesh.shape["trow"], mesh.shape["tcol"]
    in_specs = (P(None, ("clip", "trow"), "tcol"), P(), P(), P())
    out_specs = P(("clip", "trow"), "tcol")
    return jax.shard_map(
        functools.partial(body, groups, cores), mesh=mesh, in_specs=in_specs, out_specs=out_specs, check_vma=False
    )
```

```python
import functools
import math

import jax
import jax.numpy as jnp
import numpy as np
from jax import lax
from jax.experimental import pallas as pl
from jax.experimental.pallas import tpu as pltpu
from jax.sharding import PartitionSpec as P

KY = 48
LAYERS = 2
LANES = 128
HALVES = 2
QUAD = 4
TRIO = 3
XB = 32
MESH = pl.DeviceIdType.MESH
VMEM_BYTES = 62 * 1024 * 1024
BF16, F32 = jnp.bfloat16, jnp.float32
NT = (((1,), (1,)), ((), ()))


def column_constant(total, cores):
    columns = np.arange(total, dtype=np.int64)
    phase = np.arange(KY, dtype=np.int64)[:, None] * columns[None, :] % total
    angle = (phase.astype(np.float32) * np.float32(2.0 * math.pi / total)).astype(np.float64)
    table = np.concatenate([np.cos(angle), -np.sin(angle)], axis=0).astype(np.float32)
    return table.reshape(2 * KY, cores, total // cores).transpose(1, 0, 2).astype(jnp.bfloat16)


def row_constants(total, rows, groups, owners, per, sub):
    index = np.arange(owners)[:, None] * per + np.arange(sub)[None, :]
    valid = (np.arange(sub)[None, :] < per).repeat(owners, 0).reshape(-1)
    index = index.reshape(-1)
    freqs = np.where(index < KY, index, index - 2 * KY)
    keep = valid.astype(np.float64)

    def both(places):
        angle = 2.0 * math.pi * ((freqs[None, :] * places[:, None]) % total) / total
        return np.cos(angle) * keep, np.sin(angle) * keep

    fine = np.stack(both(np.arange(rows, dtype=np.int64))).astype(np.float32)
    coarse = np.stack(both(np.arange(groups, dtype=np.int64) * rows), axis=1)
    coarse = np.pad(coarse, ((0, 0), (0, 6), (0, 0))).astype(np.float32)
    return fine, coarse


def split(value):
    high = value.astype(BF16)
    return high, (value - high.astype(F32)).astype(BF16)


def turned(value):
    lane = lax.broadcasted_iota(jnp.int32, value.shape, 1)
    up = pltpu.roll(value, LANES - KY, 1)
    down = pltpu.roll(value, KY, 1)
    return jnp.where(lane < KY, up, jnp.where(lane < 2 * KY, -down, 0.0))


def pack(parts):
    lane = lax.broadcasted_iota(jnp.int32, parts[0].shape, 1)
    return [
        jnp.where(lane < 2 * KY, parts[j], pltpu.roll(parts[TRIO], 2 * KY - 32 * j, 1)) for j in range(TRIO)
    ]


def unpack(rows):
    lane = lax.broadcasted_iota(jnp.int32, rows[0].shape, 1)
    fourth = jnp.where(
        lane < 32,
        pltpu.roll(rows[0], 32, 1),
        jnp.where(lane < 64, pltpu.roll(rows[1], 64, 1), pltpu.roll(rows[2], 96, 1)),
    )
    return [jnp.where(lane < 2 * KY, r, 0.0) for r in [*rows, fourth]]


def two_transforms(table, first, second):
    value = jnp.concatenate([first, second], axis=1)
    other = jnp.concatenate([turned(first), turned(second)], axis=1)
    high, low = split(jnp.concatenate([value, other], axis=0))
    both = jnp.dot(table, jnp.concatenate([high, low, high], axis=0), preferred_element_type=F32)
    return both[:, :LANES], both[:, LANES:]


def tile_of(cols):
    for size in (2048, 1024, 512, 256, 128):
        if cols % size == 0:
            return size
    return cols


def kernel(
    plan,
    field_hbm, point_hbm, mixing_hbm, project_hbm, et_hbm, fine_hbm, coarse_hbm,
    image_out,
    value, local, et, fine, coarse, point, project, gains, gains_smem, raw, same, cross, kron, ahead, back, acc, hidden,
    total_image, packed, arrived, spread,
    field_sem, load_sem, sum_send, sum_recv, mix_send, mix_recv,
):
    groups, cores, owners, first_owner, per, sub, window, scale = plan
    channels, rows, cols = value.shape
    half_channels = channels // HALVES
    devices = groups * cores
    targets = owners * cores
    tile = tile_of(cols)
    clip = lax.axis_index("clip")
    row = lax.axis_index("trow")
    core = lax.axis_index("tcol")
    near = jnp.clip(row - first_owner, 0, owners - 1)
    is_owner = jnp.logical_and(row >= first_owner, row < first_owner + owners)
    me = row * cores + core
    block = core * owners + near
    start_mode = block * (per * KY)
    offset = lax.rem(start_mode, LANES)
    window_start = pl.multiple_of(start_mode - offset, LANES)

    loads = [
        pltpu.make_async_copy(fine_hbm, fine, load_sem.at[0]),
        pltpu.make_async_copy(coarse_hbm.at[row], coarse, load_sem.at[1]),
        pltpu.make_async_copy(et_hbm.at[core], et.at[pl.ds(0, 2 * KY)], load_sem.at[2]),
        pltpu.make_async_copy(point_hbm, point, load_sem.at[3]),
        pltpu.make_async_copy(project_hbm, project, load_sem.at[4]),
        pltpu.make_async_copy(mixing_hbm.at[:, :, :, :, pl.ds(window_start, window)], raw, load_sem.at[5]),
    ]
    for copy in loads[:3]:
        copy.start()

    def field_copy(c):
        return pltpu.make_async_copy(field_hbm.at[c], value.at[c], field_sem.at[c])

    for c in range(channels):
        field_copy(c).start()
    for copy in loads[3:]:
        copy.start()

    spread[...] = jnp.zeros_like(spread)
    et[2 * KY :, :] = jnp.zeros((LANES - 2 * KY, cols), BF16)

    def device_at(step):
        other = lax.rem(me + step, devices)
        return other // cores, lax.rem(other, cores)

    barrier = pltpu.get_barrier_semaphore()
    for step in range(1, devices):
        peer, peer_core = device_at(step)
        pl.semaphore_signal(barrier, inc=1, device_id=(clip, peer, peer_core), device_id_type=MESH)

    def used(ref):
        return ref.at[:, pl.ds(0, per), :]

    loads[0].wait()
    loads[1].wait()
    cc, cs = coarse[0:1, :], coarse[1:2, :]
    cosine = cc * fine[0] - cs * fine[1]
    sine = cs * fine[0] + cc * fine[1]
    high, low = split(jnp.concatenate([cosine, -sine], axis=1))
    back[...] = jnp.concatenate([high, high, low], axis=1)
    high, low = split(jnp.concatenate([cosine.T, sine.T], axis=1) * scale)
    ahead[...] = jnp.concatenate([high, high, low], axis=1)
    loads[2].wait()

    def columns_of(first, count):
        piece = value[first : first + count].reshape(count * rows, cols)
        result = lax.dot_general(piece, et[...], NT, preferred_element_type=F32)
        acc[first : first + count] = result.reshape(count, rows, LANES)

    def target_of(j):
        return lax.rem(near + owners // 2 + j // cores, owners), lax.rem(core + j, cores)

    def sum_copy(layer, half, j):
        q, k = target_of(j)
        slot = lax.rem(me - ((first_owner + q) * cores + k) + devices, devices) - 1
        slot = jnp.maximum(slot, 0)
        return pltpu.make_async_remote_copy(
            src_ref=used(packed.at[layer, half, k, q]),
            dst_ref=used(arrived.at[layer, half, slot]),
            send_sem=sum_send.at[layer, half, j],
            recv_sem=sum_recv.at[layer, half, slot],
            device_id=(clip, first_owner + q, k),
            device_id_type=MESH,
        )

    def for_targets(layer, half, act):
        for j in range(targets):
            q, k = target_of(j)

            @pl.when((first_owner + q) * cores + k != me)
            def _():
                act(sum_copy(layer, half, j))

    def transform_rows(layer, half):
        parts = []
        for p in range(0, half_channels, 2):
            c = half * half_channels + p
            parts.extend(two_transforms(ahead[...], acc[c], acc[c + 1]))
        for j, rows_j in enumerate(pack(parts)):
            packed[layer, half, :, :, j] = rows_j.reshape(cores, owners, sub, LANES)
        for_targets(layer, half, lambda copy: copy.start())

    def spread_copy(layer, half, step):
        peer, peer_core = device_at(step)
        return pltpu.make_async_remote_copy(
            src_ref=used(spread.at[layer, half, core, near]),
            dst_ref=used(spread.at[layer, half, core, near]),
            send_sem=mix_send.at[layer, half, step - 1],
            recv_sem=mix_recv.at[layer, half, core, near],
            device_id=(clip, peer, peer_core),
            device_id_type=MESH,
        )

    def arrival(ref, send_sem, recv_sem):
        peer, peer_core = device_at(1)
        return pltpu.make_async_remote_copy(
            src_ref=used(ref), dst_ref=used(ref), send_sem=send_sem, recv_sem=recv_sem,
            device_id=(clip, peer, peer_core), device_id_type=MESH,
        )

    order = sorted(range(1, devices), key=lambda step: abs(2 * step - devices))

    def mix(layer):
        @pl.when(is_owner)
        def _():
            plain = []
            for half in range(HALVES):
                sums = packed[layer, half, core, near]
                for slot in range(devices - 1):
                    arrival(
                        arrived.at[layer, half, slot], sum_send.at[layer, half, 0], sum_recv.at[layer, half, slot]
                    ).wait_recv()
                    sums = sums + arrived[layer, half, slot]
                plain.extend(unpack([sums[j] for j in range(TRIO)]))
            lane = lax.broadcasted_iota(jnp.int32, plain[0].shape, 1)
            swapped = [
                jnp.where(lane < KY, pltpu.roll(s, LANES - KY, 1), pltpu.roll(s, KY, 1)) for s in plain
            ]
            for half in range(HALVES):
                mixed = []
                for o in range(half * half_channels, (half + 1) * half_channels):
                    at = (layer * channels + o) * channels
                    result = same[at] * plain[0] + cross[at] * swapped[0]
                    for c in range(1, channels):
                        result = result + (same[at + c] * plain[c] + cross[at + c] * swapped[c])
                    mixed.append(result)
                for j, rows_j in enumerate(pack(mixed)):
                    spread[layer, half, core, near, j, 0:per, :] = rows_j[:per]
                for step in order:
                    spread_copy(layer, half, step).start()

    def prepare_hidden(layer, half):
        for k in range(cores):
            for q in range(owners):
                @pl.when((first_owner + q) * cores + k != me)
                def _():
                    arrival(
                        spread.at[layer, half, k, q], mix_send.at[layer, half, 0], mix_recv.at[layer, half, k, q]
                    ).wait_recv()
        parts = unpack([spread[layer, half, :, :, j].reshape(cores * owners * sub, LANES) for j in range(TRIO)])
        for p in range(0, half_channels, 2):
            for k, part in enumerate(two_transforms(back[...], parts[p], parts[p + 1])):
                hidden[half * half_channels + p + k] = part.astype(BF16)

    def kron_matrix(layer):
        size = channels * XB
        spot = lax.broadcasted_iota(jnp.int32, (size, channels), 0) // XB
        pick = (spot == lax.broadcasted_iota(jnp.int32, (size, channels), 1)).astype(F32).astype(BF16)
        wide = jnp.dot(pick, point[layer], preferred_element_type=F32).astype(BF16)
        full = lax.dot_general(wide, pick, NT, preferred_element_type=F32)
        at = lax.rem(lax.broadcasted_iota(jnp.int32, (size, size), 0), XB)
        to = lax.rem(lax.broadcasted_iota(jnp.int32, (size, size), 1), XB)
        kron[layer] = jnp.where(at == to, full, 0.0).astype(BF16)

    def mix_channels(layer):
        def step(i, carry):
            at = pl.multiple_of(i * tile, tile)
            for b in range(rows // XB):
                piece = value[:, b * XB : (b + 1) * XB, pl.ds(at, tile)].reshape(channels * XB, tile)
                result = jnp.dot(kron[layer], piece, preferred_element_type=F32)
                local[:, b * XB : (b + 1) * XB, pl.ds(at, tile)] = result.reshape(channels, XB, tile)
            return carry
        lax.fori_loop(0, cols // tile, step, 0)

    def updated(half, at, size):
        here = slice(half * half_channels, (half + 1) * half_channels)
        lhs = hidden[here].reshape(half_channels * rows, LANES)
        spectral = jnp.dot(lhs, et[:, at : at + size], preferred_element_type=F32)
        spectral = spectral.reshape(half_channels, rows, size)
        return jnp.tanh(local[here, :, at : at + size] + spectral * (1.0 / KY))

    def update(half):
        here = slice(half * half_channels, (half + 1) * half_channels)
        value[here] = updated(half, 0, cols).astype(BF16)

    def project_half(half):
        strip = min(cols, 512)
        factors = [gains_smem[0, half * half_channels + k] for k in range(half_channels)]
        for at in range(0, cols, strip):
            result = updated(half, at, strip)
            total = factors[0] * result[0]
            for k in range(1, half_channels):
                total = total + factors[k] * result[k]
            if half > 0:
                total = total_image[:, at : at + strip] + total
            if half + 1 < HALVES:
                total_image[:, at : at + strip] = total
            else:
                image_out[:, at : at + strip] = total.astype(BF16)

    def prepare_weights():
        loads[5].wait()
        count = LAYERS * 2 * channels
        flat = raw[...].astype(F32).reshape(count * channels, window).astype(BF16)
        mode = lax.broadcasted_iota(jnp.int32, (window, 2 * LANES), 0) - offset
        lane = lax.broadcasted_iota(jnp.int32, (window, 2 * LANES), 1)
        which = lane // LANES
        spot = lane - which * LANES
        wanted = which * KY + jnp.where(spot < KY, spot, spot - KY)
        wanted = jnp.where(spot < 2 * KY, wanted, -window * LANES)
        side = lax.broadcasted_iota(jnp.int32, (LAYERS * channels * channels, LANES), 1)
        for k in range(0, per, 2):
            choose = (mode - k * KY == wanted).astype(F32).astype(BF16)
            picked = jnp.dot(flat, choose, preferred_element_type=F32)
            picked = picked.reshape(LAYERS, 2, channels * channels, 2 * LANES)
            for n in range(2):
                lanes = slice(n * LANES, (n + 1) * LANES)
                real = picked[:, 0, :, lanes].reshape(LAYERS * channels * channels, LANES)
                imag = picked[:, 1, :, lanes].reshape(LAYERS * channels * channels, LANES)
                same[:, k + n, :] = real
                cross[:, k + n, :] = jnp.where(side < KY, -imag, imag)

    gain_copy = pltpu.make_async_copy(gains, gains_smem, load_sem.at[6])
    for half in range(HALVES):
        for c in range(half * half_channels, (half + 1) * half_channels, 2):
            field_copy(c).wait()
            field_copy(c + 1).wait()
            columns_of(c, 2)
        if half == 0:
            pl.semaphore_wait(barrier, devices - 1)
        transform_rows(0, half)
    loads[3].wait()
    loads[4].wait()
    gains[0:1, 0:channels] = project[...].astype(F32)
    gain_copy.start()
    for layer in range(LAYERS):
        kron_matrix(layer)
    prepare_weights()
    gain_copy.wait()

    for layer in range(LAYERS):
        last = layer + 1 == LAYERS
        if last:
            mix_channels(layer)
        mix(layer)
        if not last:
            mix_channels(layer)
        for half in range(HALVES):
            prepare_hidden(layer, half)
            if last:
                project_half(half)
            else:
                update(half)
                columns_of(half * half_channels, half_channels)
                transform_rows(layer + 1, half)

    for layer in range(LAYERS):
        for half in range(HALVES):
            for_targets(layer, half, lambda copy: copy.wait_send())

            @pl.when(is_owner)
            def _():
                for step in order:
                    spread_copy(layer, half, step).wait_send()


def body(groups, cores, field, pointwise, mixing, project):
    channels, rows, cols = field.shape
    owners = min(4, groups)
    first_owner = (groups - owners) // 2
    per = 2 * KY // (owners * cores)
    sub = -(-per // 8) * 8
    total_rows, total_cols = rows * groups, cols * cores
    scale = 1.0 / math.sqrt(total_rows * total_cols)
    modes = per * KY
    window = max(-(-(b * modes % LANES + modes) // LANES) * LANES for b in range(owners * cores))
    plan = (groups, cores, owners, first_owner, per, sub, window, scale)
    et = jnp.asarray(column_constant(total_cols, cores))
    fine, coarse = row_constants(total_rows, rows, groups, owners * cores, per, sub)
    fine, coarse = jnp.asarray(fine), jnp.asarray(coarse)

    hbm = pl.BlockSpec(memory_space=pltpu.HBM)
    dma = pltpu.SemaphoreType.DMA
    chunk = (TRIO, sub, LANES)
    pairs = LAYERS * channels * channels
    devices = groups * cores
    parts = LAYERS, HALVES
    return pl.pallas_call(
        functools.partial(kernel, plan),
        out_shape=jax.ShapeDtypeStruct((rows, cols), BF16),
        in_specs=[hbm] * 7,
        out_specs=pl.BlockSpec(memory_space=pltpu.VMEM),
        scratch_shapes=[
            pltpu.VMEM((channels, rows, cols), BF16),
            pltpu.VMEM((channels, rows, cols), F32),
            pltpu.VMEM((LANES, cols), BF16),
            pltpu.VMEM(fine.shape, F32),
            pltpu.VMEM(coarse.shape[1:], F32),
            pltpu.VMEM(pointwise.shape, BF16),
            pltpu.VMEM((1, channels), BF16),
            pltpu.VMEM((8, LANES), F32),
            pltpu.SMEM((8, LANES), F32),
            pltpu.VMEM(mixing.shape[:-1] + (window,), BF16),
            pltpu.VMEM((pairs, sub, LANES), F32),
            pltpu.VMEM((pairs, sub, LANES), F32),
            pltpu.VMEM((LAYERS, channels * XB, channels * XB), BF16),
            pltpu.VMEM((cores * owners * sub, 6 * rows), BF16),
            pltpu.VMEM((rows, 6 * cores * owners * sub), BF16),
            pltpu.VMEM((channels, rows, LANES), F32),
            pltpu.VMEM((channels, rows, LANES), BF16),
            pltpu.VMEM((rows, cols), F32),
            pltpu.VMEM(parts + (cores, owners) + chunk, F32),
            pltpu.VMEM(parts + (devices - 1,) + chunk, F32),
            pltpu.VMEM(parts + (cores, owners) + chunk, F32),
            dma((channels,)), dma((7,)),
            dma(parts + (owners * cores,)), dma(parts + (devices - 1,)),
            dma(parts + (devices - 1,)), dma(parts + (cores, owners)),
        ],
        compiler_params=pltpu.CompilerParams(
            collective_id=0, has_side_effects=True, vmem_limit_bytes=VMEM_BYTES
        ),
        name="operator",
    )(field, pointwise, mixing, project.reshape(1, channels), et, fine, coarse)


def solution(mesh):
    groups, cores = mesh.shape["trow"], mesh.shape["tcol"]
    in_specs = (P(None, ("clip", "trow"), "tcol"), P(), P(), P())
    out_specs = P(("clip", "trow"), "tcol")
    return jax.shard_map(
        functools.partial(body, groups, cores), mesh=mesh, in_specs=in_specs, out_specs=out_specs, check_vma=False
    )
```

```python
import functools
import math

import jax
import jax.numpy as jnp
import numpy as np
from jax import lax
from jax.experimental import pallas as pl
from jax.experimental.pallas import tpu as pltpu
from jax.sharding import PartitionSpec as P

KY = 48
LAYERS = 2
LANES = 128
HALVES = 2
QUAD = 4
TRIO = 3
XB = 32
MESH = pl.DeviceIdType.MESH
VMEM_BYTES = 62 * 1024 * 1024
BF16, F32 = jnp.bfloat16, jnp.float32
NT = (((1,), (1,)), ((), ()))


def column_constant(total, cores):
    columns = np.arange(total, dtype=np.int64)
    phase = np.arange(KY, dtype=np.int64)[:, None] * columns[None, :] % total
    angle = (phase.astype(np.float32) * np.float32(2.0 * math.pi / total)).astype(np.float64)
    table = np.concatenate([np.cos(angle), -np.sin(angle)], axis=0).astype(np.float32)
    return table.reshape(2 * KY, cores, total // cores).transpose(1, 0, 2).astype(jnp.bfloat16)


def row_constants(total, rows, groups, owners, per, sub):
    index = np.arange(owners)[:, None] * per + np.arange(sub)[None, :]
    valid = (np.arange(sub)[None, :] < per).repeat(owners, 0).reshape(-1)
    index = index.reshape(-1)
    freqs = np.where(index < KY, index, index - 2 * KY)
    keep = valid.astype(np.float64)

    def both(places):
        angle = 2.0 * math.pi * ((freqs[None, :] * places[:, None]) % total) / total
        return np.cos(angle) * keep, np.sin(angle) * keep

    fine = np.stack(both(np.arange(rows, dtype=np.int64))).astype(np.float32)
    coarse = np.stack(both(np.arange(groups, dtype=np.int64) * rows), axis=1)
    coarse = np.pad(coarse, ((0, 0), (0, 6), (0, 0))).astype(np.float32)
    return fine, coarse


def split(value):
    high = value.astype(BF16)
    return high, (value - high.astype(F32)).astype(BF16)


def turned(value):
    lane = lax.broadcasted_iota(jnp.int32, value.shape, 1)
    up = pltpu.roll(value, LANES - KY, 1)
    down = pltpu.roll(value, KY, 1)
    return jnp.where(lane < KY, up, jnp.where(lane < 2 * KY, -down, 0.0))


def pack(parts):
    lane = lax.broadcasted_iota(jnp.int32, parts[0].shape, 1)
    return [
        jnp.where(lane < 2 * KY, parts[j], pltpu.roll(parts[TRIO], 2 * KY - 32 * j, 1)) for j in range(TRIO)
    ]


def unpack(rows):
    lane = lax.broadcasted_iota(jnp.int32, rows[0].shape, 1)
    fourth = jnp.where(
        lane < 32,
        pltpu.roll(rows[0], 32, 1),
        jnp.where(lane < 64, pltpu.roll(rows[1], 64, 1), pltpu.roll(rows[2], 96, 1)),
    )
    return [jnp.where(lane < 2 * KY, r, 0.0) for r in [*rows, fourth]]


def two_transforms(table, first, second):
    value = jnp.concatenate([first, second], axis=1)
    other = jnp.concatenate([turned(first), turned(second)], axis=1)
    high, low = split(jnp.concatenate([value, other], axis=0))
    both = jnp.dot(table, jnp.concatenate([high, low, high], axis=0), preferred_element_type=F32)
    return both[:, :LANES], both[:, LANES:]


def tile_of(cols):
    for size in (2048, 1024, 512, 256, 128):
        if cols % size == 0:
            return size
    return cols


def kernel(
    plan,
    field_hbm, point_hbm, mixing_hbm, project_hbm, et_hbm, fine_hbm, coarse_hbm,
    image_hbm,
    value, local, et, fine, coarse, point, project, gains, gains_smem, raw, same, cross, kron, ahead, back, acc, hidden, total_image, image,
    packed, partner, mine, arrived, spread,
    field_sem, load_sem, pair_send, pair_recv, sum_send, sum_recv, mix_send, mix_recv, relay_send, relay_recv,
):
    groups, cores, owners, first_owner, per, sub, window, scale = plan
    channels, rows, cols = value.shape
    half_channels = channels // HALVES
    tile = tile_of(cols)
    local_tile = min(tile, 512)
    clip = lax.axis_index("clip")
    row = lax.axis_index("trow")
    core = lax.axis_index("tcol")
    other = 1 - core
    near = jnp.clip(row - first_owner, 0, owners - 1)
    is_owner = jnp.logical_and(row >= first_owner, row < first_owner + owners)
    block = core * owners + near
    start_mode = block * (per * KY)
    offset = lax.rem(start_mode, LANES)
    window_start = pl.multiple_of(start_mode - offset, LANES)

    loads = [
        pltpu.make_async_copy(fine_hbm, fine, load_sem.at[0]),
        pltpu.make_async_copy(coarse_hbm.at[row], coarse, load_sem.at[1]),
        pltpu.make_async_copy(et_hbm.at[core], et.at[pl.ds(0, 2 * KY)], load_sem.at[2]),
        pltpu.make_async_copy(point_hbm, point, load_sem.at[3]),
        pltpu.make_async_copy(project_hbm, project, load_sem.at[4]),
        pltpu.make_async_copy(mixing_hbm.at[:, :, :, :, pl.ds(window_start, window)], raw, load_sem.at[5]),
    ]
    for copy in loads[:3]:
        copy.start()

    def field_copy(c):
        return pltpu.make_async_copy(field_hbm.at[c], value.at[c], field_sem.at[c])

    for c in range(channels):
        field_copy(c).start()
    for copy in loads[3:]:
        copy.start()

    spread[...] = jnp.zeros_like(spread)
    et[2 * KY :, :] = jnp.zeros((LANES - 2 * KY, cols), BF16)

    barrier = pltpu.get_barrier_semaphore()
    pl.semaphore_signal(barrier, inc=1, device_id=(clip, row, other), device_id_type=MESH)
    for j in range(1, groups):
        peer = lax.rem(row + j, groups)
        pl.semaphore_signal(barrier, inc=1, device_id=(clip, peer, core), device_id_type=MESH)

    def used(ref):
        return ref.at[:, pl.ds(0, per), :]

    loads[0].wait()
    loads[1].wait()
    cc, cs = coarse[0:1, :], coarse[1:2, :]
    cosine = cc * fine[0] - cs * fine[1]
    sine = cs * fine[0] + cc * fine[1]
    high, low = split(jnp.concatenate([cosine, -sine], axis=1))
    back[...] = jnp.concatenate([high, high, low], axis=1)
    high, low = split(jnp.concatenate([cosine.T, sine.T], axis=1) * scale)
    ahead[...] = jnp.concatenate([high, high, low], axis=1)
    loads[2].wait()

    def columns_of(c):
        acc[c] = lax.dot_general(value[c], et[...], NT, preferred_element_type=F32)

    def pair_copy(layer, half):
        return pltpu.make_async_remote_copy(
            src_ref=packed.at[layer, half, other],
            dst_ref=partner.at[layer, half],
            send_sem=pair_send.at[layer, half],
            recv_sem=pair_recv.at[layer, half],
            device_id=(clip, row, other),
            device_id_type=MESH,
        )

    def transform_rows(layer, half):
        parts = []
        for p in range(0, half_channels, 2):
            c = half * half_channels + p
            parts.extend(two_transforms(ahead[...], acc[c], acc[c + 1]))
        for j, rows_j in enumerate(pack(parts)):
            packed[layer, half, :, :, j] = rows_j.reshape(cores, owners, sub, LANES)
        pair_copy(layer, half).start()

    def sum_target(j):
        return lax.rem(near + owners // 2 + j, owners)

    def sum_copy(layer, half, j):
        q = sum_target(j)
        slot = lax.rem(row - (first_owner + q) + groups, groups) - 1
        slot = jnp.maximum(slot, 0)
        return pltpu.make_async_remote_copy(
            src_ref=used(mine.at[layer, half, q]),
            dst_ref=used(arrived.at[layer, half, slot]),
            send_sem=sum_send.at[layer, half, j],
            recv_sem=sum_recv.at[layer, half, slot],
            device_id=(clip, first_owner + q, core),
            device_id_type=MESH,
        )

    def scatter_sums(layer, half):
        pair_copy(layer, half).wait_recv()
        mine[layer, half] = packed[layer, half, core] + partner[layer, half]
        for j in range(owners):
            @pl.when(first_owner + sum_target(j) != row)
            def _():
                sum_copy(layer, half, j).start()

    def spread_copy(layer, half, j):
        return pltpu.make_async_remote_copy(
            src_ref=used(spread.at[layer, half, core, near]),
            dst_ref=used(spread.at[layer, half, core, near]),
            send_sem=mix_send.at[layer, half, j - 1],
            recv_sem=mix_recv.at[layer, half, near],
            device_id=(clip, lax.rem(row + j, groups), core),
            device_id_type=MESH,
        )

    def relay_copy(layer, half, q):
        return pltpu.make_async_remote_copy(
            src_ref=used(spread.at[layer, half, core, q]),
            dst_ref=used(spread.at[layer, half, core, q]),
            send_sem=relay_send.at[layer, half, q],
            recv_sem=relay_recv.at[layer, half, q],
            device_id=(clip, row, other),
            device_id_type=MESH,
        )

    def block_arrival(layer, half, q):
        return pltpu.make_async_remote_copy(
            src_ref=used(spread.at[layer, half, core, q]),
            dst_ref=used(spread.at[layer, half, core, q]),
            send_sem=mix_send.at[layer, half, 0],
            recv_sem=mix_recv.at[layer, half, q],
            device_id=(clip, row, other),
            device_id_type=MESH,
        )

    def partner_arrival(layer, half, q):
        return pltpu.make_async_remote_copy(
            src_ref=used(spread.at[layer, half, other, q]),
            dst_ref=used(spread.at[layer, half, other, q]),
            send_sem=relay_send.at[layer, half, q],
            recv_sem=relay_recv.at[layer, half, q],
            device_id=(clip, row, other),
            device_id_type=MESH,
        )

    def sum_arrival(layer, half, slot):
        return pltpu.make_async_remote_copy(
            src_ref=used(arrived.at[layer, half, slot]),
            dst_ref=used(arrived.at[layer, half, slot]),
            send_sem=sum_send.at[layer, half, 0],
            recv_sem=sum_recv.at[layer, half, slot],
            device_id=(clip, row, other),
            device_id_type=MESH,
        )

    order = sorted(range(1, groups), key=lambda j: abs(2 * j - groups))

    def mix(layer):
        @pl.when(is_owner)
        def _():
            plain = []
            for half in range(HALVES):
                sums = mine[layer, half, near]
                for slot in range(groups - 1):
                    sum_arrival(layer, half, slot).wait_recv()
                    sums = sums + arrived[layer, half, slot]
                plain.extend(unpack([sums[j] for j in range(TRIO)]))
            lane = lax.broadcasted_iota(jnp.int32, plain[0].shape, 1)
            swapped = [
                jnp.where(lane < KY, pltpu.roll(s, LANES - KY, 1), pltpu.roll(s, KY, 1)) for s in plain
            ]
            for half in range(HALVES):
                mixed = []
                for o in range(half * half_channels, (half + 1) * half_channels):
                    at = (layer * channels + o) * channels
                    result = same[at] * plain[0] + cross[at] * swapped[0]
                    for c in range(1, channels):
                        result = result + (same[at + c] * plain[c] + cross[at + c] * swapped[c])
                    mixed.append(result)
                for j, rows_j in enumerate(pack(mixed)):
                    spread[layer, half, core, near, j, 0:per, :] = rows_j[:per]
                for j in order:
                    spread_copy(layer, half, j).start()
                relay_copy(layer, half, near).start()

    def relay(layer, half):
        for q in range(owners):
            @pl.when(first_owner + q != row)
            def _():
                block_arrival(layer, half, q).wait_recv()
                relay_copy(layer, half, q).start()

    def prepare_hidden(layer, half):
        for q in range(owners):
            partner_arrival(layer, half, q).wait_recv()
        parts = unpack([spread[layer, half, :, :, j].reshape(cores * owners * sub, LANES) for j in range(TRIO)])
        for p in range(0, half_channels, 2):
            for k, part in enumerate(two_transforms(back[...], parts[p], parts[p + 1])):
                hidden[half * half_channels + p + k] = part.astype(BF16)

    def kron_matrix(layer):
        size = channels * XB
        spot = lax.broadcasted_iota(jnp.int32, (size, channels), 0) // XB
        pick = (spot == lax.broadcasted_iota(jnp.int32, (size, channels), 1)).astype(F32).astype(BF16)
        wide = jnp.dot(pick, point[layer], preferred_element_type=F32).astype(BF16)
        full = lax.dot_general(wide, pick, NT, preferred_element_type=F32)
        at = lax.rem(lax.broadcasted_iota(jnp.int32, (size, size), 0), XB)
        to = lax.rem(lax.broadcasted_iota(jnp.int32, (size, size), 1), XB)
        kron[layer] = jnp.where(at == to, full, 0.0).astype(BF16)

    def mix_channels(layer):
        def step(i, carry):
            at = pl.multiple_of(i * local_tile, local_tile)
            for b in range(rows // XB):
                piece = value[:, b * XB : (b + 1) * XB, pl.ds(at, local_tile)].reshape(channels * XB, local_tile)
                result = jnp.dot(kron[layer], piece, preferred_element_type=F32)
                local[:, b * XB : (b + 1) * XB, pl.ds(at, local_tile)] = result.reshape(channels, XB, local_tile)
            return carry
        lax.fori_loop(0, cols // local_tile, step, 0)

    def half_slice(half):
        return pl.ds(half * half_channels, half_channels)

    def updated(half, at):
        lhs = hidden[half_slice(half)].reshape(half_channels * rows, LANES)
        spectral = jnp.dot(lhs, et[:, pl.ds(at, tile)], preferred_element_type=F32)
        spectral = spectral.reshape(half_channels, rows, tile)
        return jnp.tanh(local[half_slice(half), :, pl.ds(at, tile)] + spectral * (1.0 / KY))

    def update(half):
        def step(i, carry):
            at = pl.multiple_of(i * tile, tile)
            value[half_slice(half), :, pl.ds(at, tile)] = updated(half, at).astype(BF16)
            return carry
        lax.fori_loop(0, cols // tile, step, 0)

    def project_half(half):
        factors = [gains_smem[0, half * half_channels + k] for k in range(half_channels)]

        def step(i, carry):
            at = pl.multiple_of(i * tile, tile)
            result = updated(half, at)
            total = total_image[:, pl.ds(at, tile)]
            for k in range(half_channels):
                total = total + factors[k] * result[k]
            total_image[:, pl.ds(at, tile)] = total
            image[:, pl.ds(at, tile)] = total.astype(BF16)
            return carry
        lax.fori_loop(0, cols // tile, step, 0)

    def prepare_weights():
        loads[5].wait()
        count = LAYERS * 2 * channels
        flat = raw[...].astype(F32).reshape(count * channels, window).astype(BF16)
        mode = lax.broadcasted_iota(jnp.int32, (window, 2 * LANES), 0) - offset
        lane = lax.broadcasted_iota(jnp.int32, (window, 2 * LANES), 1)
        which = lane // LANES
        spot = lane - which * LANES
        wanted = which * KY + jnp.where(spot < KY, spot, spot - KY)
        wanted = jnp.where(spot < 2 * KY, wanted, -window * LANES)
        side = lax.broadcasted_iota(jnp.int32, (LAYERS * channels * channels, LANES), 1)
        for k in range(0, per, 2):
            choose = (mode - k * KY == wanted).astype(F32).astype(BF16)
            picked = jnp.dot(flat, choose, preferred_element_type=F32)
            picked = picked.reshape(LAYERS, 2, channels * channels, 2 * LANES)
            for n in range(2):
                lanes = slice(n * LANES, (n + 1) * LANES)
                real = picked[:, 0, :, lanes].reshape(LAYERS * channels * channels, LANES)
                imag = picked[:, 1, :, lanes].reshape(LAYERS * channels * channels, LANES)
                same[:, k + n, :] = real
                cross[:, k + n, :] = jnp.where(side < KY, -imag, imag)

    gain_copy = pltpu.make_async_copy(gains, gains_smem, load_sem.at[6])

    def load_and_transform(c, carry):
        field_copy(c).wait()
        columns_of(c)
        return carry

    def transform_only(c, carry):
        columns_of(c)
        return carry

    def first_half(half, carry):
        first = half * half_channels
        lax.fori_loop(first, first + half_channels, load_and_transform, 0)

        @pl.when(half == 0)
        def _():
            pl.semaphore_wait(barrier, groups)

        @pl.when(half > 0)
        def _():
            scatter_sums(0, 0)
        transform_rows(0, half)
        return carry

    lax.fori_loop(0, HALVES, first_half, 0)
    loads[3].wait()
    loads[4].wait()
    gains[0:1, 0:channels] = project[...].astype(F32)
    gain_copy.start()
    total_image[...] = jnp.zeros_like(total_image)

    def prepare_kron(layer, carry):
        kron_matrix(layer)
        return carry

    lax.fori_loop(0, LAYERS, prepare_kron, 0)
    scatter_sums(0, 1)
    prepare_weights()
    gain_copy.wait()

    def one_layer(layer, carry):
        mix(layer)
        mix_channels(layer)
        relay(layer, 0)

        def one_half(half, inner):
            prepare_hidden(layer, half)

            @pl.when(layer + 1 == LAYERS)
            def _():
                project_half(half)

            @pl.when(layer + 1 < LAYERS)
            def _():
                update(half)

            @pl.when(half == 0)
            def _():
                relay(layer, 1)

            @pl.when(layer + 1 < LAYERS)
            def _():
                @pl.when(half > 0)
                def _():
                    scatter_sums(layer + 1, 0)
                first = half * half_channels
                lax.fori_loop(first, first + half_channels, transform_only, 0)
                transform_rows(layer + 1, half)
            return inner

        lax.fori_loop(0, HALVES, one_half, 0)

        @pl.when(layer + 1 < LAYERS)
        def _():
            scatter_sums(layer + 1, 1)
        return carry

    lax.fori_loop(0, LAYERS, one_layer, 0)

    out = pltpu.make_async_copy(image, image_hbm, load_sem.at[6])
    out.start()
    def drain(n, carry):
        layer, half = n // HALVES, lax.rem(n, HALVES)
        pair_copy(layer, half).wait_send()
        for j in range(owners):
            @pl.when(first_owner + sum_target(j) != row)
            def _():
                sum_copy(layer, half, j).wait_send()
        for q in range(owners):
            relay_copy(layer, half, q).wait_send()

        @pl.when(is_owner)
        def _():
            for j in order:
                spread_copy(layer, half, j).wait_send()
        return carry

    lax.fori_loop(0, LAYERS * HALVES, drain, 0)
    out.wait()


def body(groups, cores, field, pointwise, mixing, project):
    channels, rows, cols = field.shape
    owners = min(4, groups)
    first_owner = (groups - owners) // 2
    per = 2 * KY // (owners * cores)
    sub = -(-per // 8) * 8
    total_rows, total_cols = rows * groups, cols * cores
    scale = 1.0 / math.sqrt(total_rows * total_cols)
    modes = per * KY
    window = max(-(-(b * modes % LANES + modes) // LANES) * LANES for b in range(owners * cores))
    plan = (groups, cores, owners, first_owner, per, sub, window, scale)
    et = jnp.asarray(column_constant(total_cols, cores))
    fine, coarse = row_constants(total_rows, rows, groups, owners * cores, per, sub)
    fine, coarse = jnp.asarray(fine), jnp.asarray(coarse)

    hbm = pl.BlockSpec(memory_space=pl.ANY)
    dma = pltpu.SemaphoreType.DMA
    links = max(groups - 1, 1)
    chunk = (TRIO, sub, LANES)
    pairs = LAYERS * channels * channels
    return pl.pallas_call(
        functools.partial(kernel, plan),
        out_shape=jax.ShapeDtypeStruct((rows, cols), BF16),
        in_specs=[hbm] * 7,
        out_specs=hbm,
        scratch_shapes=[
            pltpu.VMEM((channels, rows, cols), BF16),
            pltpu.VMEM((channels, rows, cols), F32),
            pltpu.VMEM((LANES, cols), BF16),
            pltpu.VMEM(fine.shape, F32),
            pltpu.VMEM(coarse.shape[1:], F32),
            pltpu.VMEM(pointwise.shape, BF16),
            pltpu.VMEM((1, channels), BF16),
            pltpu.VMEM((8, LANES), F32),
            pltpu.SMEM((8, LANES), F32),
            pltpu.VMEM(mixing.shape[:-1] + (window,), BF16),
            pltpu.VMEM((pairs, sub, LANES), F32),
            pltpu.VMEM((pairs, sub, LANES), F32),
            pltpu.VMEM((LAYERS, channels * XB, channels * XB), BF16),
            pltpu.VMEM((cores * owners * sub, 6 * rows), BF16),
            pltpu.VMEM((rows, 6 * cores * owners * sub), BF16),
            pltpu.VMEM((channels, rows, LANES), F32),
            pltpu.VMEM((channels, rows, LANES), BF16),
            pltpu.VMEM((rows, cols), F32),
            pltpu.VMEM((rows, cols), BF16),
            pltpu.VMEM((LAYERS, HALVES, cores, owners) + chunk, F32),
            pltpu.VMEM((LAYERS, HALVES, owners) + chunk, F32),
            pltpu.VMEM((LAYERS, HALVES, owners) + chunk, F32),
            pltpu.VMEM((LAYERS, HALVES, links) + chunk, F32),
            pltpu.VMEM((LAYERS, HALVES, cores, owners) + chunk, F32),
            dma((channels,)), dma((7,)),
            dma((LAYERS, HALVES)), dma((LAYERS, HALVES)),
            dma((LAYERS, HALVES, owners)), dma((LAYERS, HALVES, links)),
            dma((LAYERS, HALVES, links)), dma((LAYERS, HALVES, owners)),
            dma((LAYERS, HALVES, owners)), dma((LAYERS, HALVES, owners)),
        ],
        compiler_params=pltpu.CompilerParams(
            collective_id=0, has_side_effects=True, vmem_limit_bytes=VMEM_BYTES
        ),
        name="operator",
    )(field, pointwise, mixing, project.reshape(1, channels), et, fine, coarse)


def solution(mesh):
    groups, cores = mesh.shape["trow"], mesh.shape["tcol"]
    in_specs = (P(None, ("clip", "trow"), "tcol"), P(), P(), P())
    out_specs = P(("clip", "trow"), "tcol")
    return jax.shard_map(
        functools.partial(body, groups, cores), mesh=mesh, in_specs=in_specs, out_specs=out_specs, check_vma=False
    )
```
